256 devices in a mesh: grp: 8 (over y, core), shard: 32 (over z, x).
Axes of the slice: x: 4, y: 4, z: 8, core: 2. Of those that a mesh axis runs over, the one named last changes fastest.
Arguments:
- regressors: bfloat16 [786432, 512], P(('grp', 'shard')), may hold values from -40 to 40
- targets: bfloat16 [786432, 512], P(('grp', 'shard')), may hold values from -120 to 120
Outputs:
- predictor: float32 [512, 512], replicated
- residuals: bfloat16 [786432, 512], P(('grp', 'shard'))
The draws below stay inside these ranges and needn't reach their ends.
All inputs are finite; a program needn't handle non-finite values.
Results may differ from the reference program's by a relative error of at most 0.0013.
Values sent between devices are 32-bit elements; how exact they have to be, the bound alone decides.
No kernel may reach another device: no remote copies, remote signals or barrier semaphores. Data moves between devices by JAX's collectives and lax.ppermute only.
A program may use at most 64 MiB of HBM per device.

```python
import math
import jax
import jax.numpy as jnp
from jax import lax

K = 512
P_SIZE = 512
ROWS_DEV = 3072
ROWS = 786432
N_GRP = 8
N_SHARD = 32


def telemetry(key):
    times = jnp.arange(ROWS, dtype=jnp.float32) / ROWS
    trend = jnp.exp(math.log(3.0) * times)
    mixing = 0.8
    factor_row = jnp.exp(jax.random.uniform(jax.random.fold_in(key, 11), (ROWS,), jnp.float32, math.log(0.5), math.log(2.0)))
    fresh = jnp.clip(jax.random.normal(jax.random.fold_in(key, 12), (ROWS, K), jnp.float32), -4.5, 4.5)
    base = (fresh + mixing * jnp.roll(fresh, 1, axis=1)) / math.sqrt(1.0 + mixing * mixing)
    amplitude = trend * factor_row
    modes = base * amplitude[:, None]
    coeff_mean = jax.random.uniform(jax.random.fold_in(key, 21), (P_SIZE,), jnp.float32, -1.0, 1.0)
    coeff_swing = jax.random.uniform(jax.random.fold_in(key, 22), (P_SIZE,), jnp.float32, 0.3, 0.8)
    phases = jax.random.uniform(jax.random.fold_in(key, 23), (P_SIZE,), jnp.float32, 0.0, 1.0)
    coupling = jax.random.uniform(jax.random.fold_in(key, 24), (P_SIZE,), jnp.float32, -0.5, 0.5)
    coeff_now = coeff_mean[None, :] + coeff_swing[None, :] * jnp.sin(2.0 * math.pi * (phases[None, :] + 3.0 * times[:, None]))
    neighbour = jnp.roll(modes, -1, axis=1)[:, :P_SIZE]
    noise_part = 0.5 * jnp.clip(jax.random.normal(jax.random.fold_in(key, 25), (ROWS, P_SIZE), jnp.float32), -4.5, 4.5) * amplitude[:, None]
    future = coeff_now * modes[:, :P_SIZE] + coupling[None, :] * neighbour + noise_part
    return (modes, future)


def draw_regressors(key, part):
    return telemetry(key)[0].astype(jnp.bfloat16)


def draw_targets(key, part):
    return telemetry(key)[1].astype(jnp.bfloat16)


def setup_inputs(seed: int = 0) -> dict:
    seeds = jax.random.split(jax.random.key(seed), 3)
    return {
        "regressors": draw_regressors(jax.random.fold_in(seeds[2], 71), 0),
        "targets": draw_targets(jax.random.fold_in(seeds[2], 71), 0),
    }


def solve_predictor(factor, cross_sum):
    interim = jax.scipy.linalg.solve_triangular(factor, cross_sum, lower=True)
    return jax.scipy.linalg.solve_triangular(factor, interim, lower=True, trans=1)

def residual_block(rows_x, rows_y, predictor):
    pred_high = predictor.astype(jnp.bfloat16)
    pred_low = (predictor - lax.optimization_barrier(pred_high).astype(jnp.float32)).astype(jnp.bfloat16)
    estimate = jnp.dot(rows_x.astype(jnp.float32), pred_high.astype(jnp.float32), preferred_element_type=jnp.float32) + jnp.dot(rows_x.astype(jnp.float32), pred_low.astype(jnp.float32), preferred_element_type=jnp.float32)
    return (rows_y.astype(jnp.float32) - estimate).astype(jnp.bfloat16)

def reference(regressors, targets):
    gram_total = jnp.dot(regressors.T.astype(jnp.float32), regressors.astype(jnp.float32), preferred_element_type=jnp.float32)
    cross_total = jnp.dot(regressors.T.astype(jnp.float32), targets.astype(jnp.float32), preferred_element_type=jnp.float32)
    factor = jnp.linalg.cholesky(gram_total)
    predictor = solve_predictor(factor, cross_total)
    blocks_x = regressors.reshape(N_GRP * N_SHARD, ROWS_DEV, K)
    blocks_y = targets.reshape(N_GRP * N_SHARD, ROWS_DEV, P_SIZE)
    residuals = lax.map(lambda pair: residual_block(pair[0], pair[1], predictor), (blocks_x, blocks_y))
    return (predictor, residuals.reshape(ROWS, P_SIZE))
```

```python
import functools

import jax
import jax.numpy as jnp
from jax import lax
from jax.experimental import pallas as pl
from jax.experimental.pallas import tpu as pltpu
from jax.sharding import PartitionSpec as P


F32 = jnp.float32
HI = lax.Precision.HIGHEST
K = 512
HALF = 256
NB = 128
STEP = 512
CHUNK = 512
NY = 4
NZX = 32


def sums_kernel(where_ref, x_ref, y_ref, out_ref, acc_ref):
    step = pl.program_id(0)
    col = pl.multiple_of(where_ref[0] * HALF, HALF)
    contract = (((0,), (0,)), ((), ()))
    both = jnp.concatenate([x_ref[:, pl.ds(col, HALF)], y_ref[...]], axis=1)
    part = lax.dot_general(x_ref[...], both, contract, preferred_element_type=F32)

    @pl.when(step == 0)
    def _():
        acc_ref[...] = part

    @pl.when(step > 0)
    def _():
        acc_ref[...] += part

    @pl.when(step == pl.num_programs(0) - 1)
    def _():
        for kind in range(2):
            for jj in range(2):
                for ih in range(2):
                    c0 = kind * HALF + jj * NB
                    tile = acc_ref[HALF * ih : HALF * (ih + 1), c0 : c0 + NB]
                    out_ref[jj * 2 + ih, :, kind] = tile.reshape(NZX, 8, NB)


def local_sums(half, x, y):
    rows = x.shape[0]
    return pl.pallas_call(
        sums_kernel,
        grid_spec=pltpu.PrefetchScalarGridSpec(
            num_scalar_prefetch=1,
            grid=(rows // STEP,),
            in_specs=[
                pl.BlockSpec((STEP, K), lambda i, w: (i, 0)),
                pl.BlockSpec((STEP, HALF), lambda i, w: (i, w[0])),
            ],
            out_specs=pl.BlockSpec((NY, NZX, 2, 8, NB), lambda i, w: (0, 0, 0, 0, 0)),
            scratch_shapes=[pltpu.VMEM((K, 2 * HALF), F32)],
        ),
        out_shape=jax.ShapeDtypeStruct((NY, NZX, 2, 8, NB), F32),
        compiler_params=pltpu.CompilerParams(dimension_semantics=("arbitrary",)),
        cost_estimate=pl.CostEstimate(
            flops=2 * rows * K * K, bytes_accessed=rows * K * 4, transcendentals=0
        ),
        name="local_sums",
    )(half, x, y)


def lane_bcast(v, c):
    return jnp.broadcast_to(v[:, c : c + 1], (8, NB))


def sub_bcast(v, r):
    return jnp.broadcast_to(v[r : r + 1, :], (8, NB))


def inverse_128(rows):
    sub = lax.broadcasted_iota(jnp.int32, (8, NB), 0)
    lane = lax.broadcasted_iota(jnp.int32, (8, NB), 1)
    rows = list(rows)
    for p in range(16):
        o = 8 * p
        panel = rows[p]
        cols = [lane_bcast(panel, o + j) for j in range(8)]
        inside = (lane >= o) & (lane < o + 8)
        panel = jnp.where(inside, jnp.where(lane - o == sub, 1.0, 0.0), panel)
        for j in range(8):
            on_pivot = sub == j
            r = 1.0 / sub_bcast(cols[j], j)
            m = cols[j] * r

            def eliminate(v):
                pivot_row = sub_bcast(v, j)
                return jnp.where(on_pivot, pivot_row * r, v - m * pivot_row)

            for q in range(j + 1, 8):
                cols[q] = eliminate(cols[q])
            panel = eliminate(panel)
        rows[p] = panel
        pivots = [sub_bcast(panel, j) for j in range(8)]
        for t in range(15):
            i = (p + 1 + t) % 16
            v = rows[i]
            terms = [lane_bcast(v, o + j) * pivots[j] for j in range(8)]
            while len(terms) > 1:
                terms = [terms[s] + terms[s + 1] for s in range(0, len(terms), 2)]
            rows[i] = jnp.where(inside, 0.0, v) - terms[0]
    return rows


def invert(a_ref):
    nb = K // NB
    blk = lambda k: slice(NB * k, NB * (k + 1))
    for k in range(nb):
        ks = blk(k)
        rows = inverse_128([a_ref[NB * k + 8 * t : NB * k + 8 * t + 8, ks] for t in range(16)])
        diag = jnp.concatenate(rows, axis=0)
        right = {}
        for j in range(nb):
            if j == k:
                right[j] = diag
            else:
                right[j] = jnp.dot(diag, a_ref[ks, blk(j)], precision=HI, preferred_element_type=F32)
        left = {i: a_ref[blk(i), ks] for i in range(nb) if i != k}
        for j in range(nb):
            a_ref[ks, blk(j)] = right[j]
        for s in range(nb - 1):
            i = (k + 1 + s) % nb
            for t in range(nb):
                j = (k + 1 + t) % nb
                u = jnp.dot(left[i], right[j], precision=HI, preferred_element_type=F32)
                if j == k:
                    a_ref[blk(i), ks] = -u
                else:
                    a_ref[blk(i), blk(j)] = a_ref[blk(i), blk(j)] - u


def solve_kernel(where_ref, *refs):
    pieces = refs[:8]
    x_hbm, y_hbm, pred_ref, res_hbm = refs[8:12]
    a_ref, c_ref, x_ref, y_ref, res_ref, hi_ref, lo_ref, sem_x, sem_y, sem_o = refs[12:]
    load_x = pltpu.make_async_copy(x_hbm, x_ref, sem_x)
    load_y = pltpu.make_async_copy(y_hbm, y_ref, sem_y)
    load_x.start()
    load_y.start()
    core, y = where_ref[0], where_ref[1]
    for side in range(2):
        half = core if side == 0 else 1 - core
        for d in range(NY):
            piece = pieces[side * NY + d]
            part = lax.rem(y + (NY - d), NY)
            row = pl.multiple_of(lax.rem(part, 2) * HALF, HALF)
            col = pl.multiple_of((half * 2 + lax.div(part, 2)) * NB, NB)
            a_ref[pl.ds(row, HALF), pl.ds(col, NB)] = piece[:, 0].reshape(HALF, NB)
            c_ref[pl.ds(row, HALF), pl.ds(col, NB)] = piece[:, 1].reshape(HALF, NB)
    invert(a_ref)
    pred = jnp.dot(a_ref[...], c_ref[...], precision=HI, preferred_element_type=F32)
    pred_ref[...] = pred
    high = pred.astype(jnp.bfloat16)
    hi_ref[...] = high
    lo_ref[...] = (pred - high.astype(F32)).astype(jnp.bfloat16)
    load_x.wait()
    load_y.wait()
    stores = []
    for n in range(res_ref.shape[0] // CHUNK):
        rows = slice(n * CHUNK, (n + 1) * CHUNK)
        x = x_ref[rows, :]
        estimate = jnp.dot(x, hi_ref[...], preferred_element_type=F32) + jnp.dot(
            x, lo_ref[...], preferred_element_type=F32
        )
        res_ref[rows, :] = (y_ref[rows, :].astype(F32) - estimate).astype(jnp.bfloat16)
        store = pltpu.make_async_copy(res_ref.at[rows, :], res_hbm.at[rows, :], sem_o.at[n])
        store.start()
        stores.append(store)
    for store in stores:
        store.wait()


def solve(where, pieces, x, y):
    rows = x.shape[0]
    vmem = pl.BlockSpec(memory_space=pltpu.VMEM)
    hbm = pl.BlockSpec(memory_space=pl.ANY)
    return pl.pallas_call(
        solve_kernel,
        in_specs=[pl.BlockSpec(memory_space=pltpu.SMEM)] + [vmem] * 8 + [hbm] * 2,
        out_specs=(vmem, hbm),
        out_shape=(
            jax.ShapeDtypeStruct((K, K), F32),
            jax.ShapeDtypeStruct((rows, K), jnp.bfloat16),
        ),
        scratch_shapes=[
            pltpu.VMEM((K, K), F32),
            pltpu.VMEM((K, K), F32),
            pltpu.VMEM((rows, K), jnp.bfloat16),
            pltpu.VMEM((rows, K), jnp.bfloat16),
            pltpu.VMEM((rows, K), jnp.bfloat16),
            pltpu.VMEM((K, K), jnp.bfloat16),
            pltpu.VMEM((K, K), jnp.bfloat16),
            pltpu.SemaphoreType.DMA,
            pltpu.SemaphoreType.DMA,
            pltpu.SemaphoreType.DMA((rows // CHUNK,)),
        ],
        name="solve",
    )(where, *pieces, x, y)


def body(regressors, targets):
    grp = lax.axis_index("grp")
    core, y = grp % 2, grp // 2
    other = [(g, g ^ 1) for g in range(8)]
    same_core = [[0, 2, 4, 6], [1, 3, 5, 7]]

    sent = local_sums(jnp.full((1,), 1 - core, jnp.int32), regressors, targets)
    taken = lax.ppermute(sent, "grp", other)
    kept = local_sums(jnp.full((1,), core, jnp.int32), regressors, targets)
    chip = kept + taken
    by_y = lax.all_to_all(chip, "grp", 0, 0, axis_index_groups=same_core, tiled=True)
    column = by_y.sum(axis=0)
    by_zx = lax.all_to_all(column, "shard", 0, 0, tiled=True)
    tile = by_zx.sum(axis=0)
    mine = lax.all_to_all(
        jnp.broadcast_to(tile, (NZX, 2, 8, NB)), "shard", 0, 0, tiled=True
    )
    near = [mine] + [
        lax.ppermute(mine, "grp", [(g, (g + 2 * d) % 8) for g in range(8)]) for d in range(1, NY)
    ]
    far = [lax.ppermute(piece, "grp", other) for piece in near]
    where = jnp.stack([core, y]).astype(jnp.int32)
    return solve(where, near + far, regressors, targets)


def solution(mesh):
    placed = (P(("grp", "shard"), None), P(("grp", "shard"), None))
    return jax.shard_map(
        body,
        mesh=mesh,
        in_specs=placed,
        out_specs=(P(), P(("grp", "shard"), None)),
        check_vma=False,
    )
```

```python
import functools

import jax
import jax.numpy as jnp
from jax import lax
from jax.experimental import pallas as pl
from jax.experimental.pallas import tpu as pltpu
from jax.sharding import PartitionSpec as P


F32 = jnp.float32
HI = lax.Precision.HIGHEST
K = 512
HALF = 256
NB = 128
CHUNK = 512
NY = 4
NZX = 32


def sums_kernel(where_ref, x_ref, z_ref, send_ref, keep_ref, next_ref, _, acc_ref):
    next_ref[0] = where_ref[0]
    next_ref[1] = where_ref[1]
    acc_ref[...] = lax.dot_general(
        x_ref[...], z_ref[...], (((0,), (0,)), ((), ())), preferred_element_type=F32
    )
    core = where_ref[0]
    for out_ref, half in ((send_ref, 1 - core), (keep_ref, core)):
        for jj in range(2):
            col = pl.multiple_of(half * HALF + jj * NB, NB)
            for ih in range(2):
                tile = acc_ref[HALF * ih : HALF * (ih + 1), pl.ds(col, NB)]
                out_ref[jj * 2 + ih] = tile.reshape(NZX, 8, NB)


def local_sums(where, x, z, name):
    vmem = pl.BlockSpec(memory_space=pltpu.VMEM)
    out_shape = jax.ShapeDtypeStruct((NY, NZX, 8, NB), F32)
    return pl.pallas_call(
        sums_kernel,
        in_specs=[pl.BlockSpec(memory_space=pltpu.SMEM), vmem, vmem],
        out_specs=(vmem, vmem, pl.BlockSpec(memory_space=pltpu.SMEM), vmem),
        out_shape=(
            out_shape,
            out_shape,
            jax.ShapeDtypeStruct((2,), jnp.int32),
            jax.ShapeDtypeStruct(x.shape, x.dtype),
        ),
        input_output_aliases={1: 3},
        scratch_shapes=[pltpu.VMEM((K, K), F32)],
        compiler_params=pltpu.CompilerParams(vmem_limit_bytes=24 << 20),
        cost_estimate=pl.CostEstimate(
            flops=2 * x.shape[0] * K * K, bytes_accessed=8 << 20, transcendentals=0
        ),
        name=name,
    )(where, x, z)


def chip_kernel(where_ref, keep_g, keep_c, taken_g, taken_c, *out_refs):
    for d in range(NY):
        part = lax.rem(where_ref[1] + d, NY)
        out_refs[d][:, 0] = keep_g[part] + taken_g[part]
        out_refs[d][:, 1] = keep_c[part] + taken_c[part]


def chip_sums(where, *parts):
    vmem = pl.BlockSpec(memory_space=pltpu.VMEM)
    return pl.pallas_call(
        chip_kernel,
        in_specs=[pl.BlockSpec(memory_space=pltpu.SMEM)] + [vmem] * 4,
        out_specs=(vmem,) * NY,
        out_shape=(jax.ShapeDtypeStruct((NZX, 2, 8, NB), F32),) * NY,
        compiler_params=pltpu.CompilerParams(vmem_limit_bytes=8 << 20),
        name="chip_sums",
    )(where, *parts)


def lane_bcast(v, c):
    return jnp.broadcast_to(v[:, c : c + 1], (8, NB))


def sub_bcast(v, r):
    return jnp.broadcast_to(v[r : r + 1, :], (8, NB))


def inverse_128(rows):
    sub = lax.broadcasted_iota(jnp.int32, (8, NB), 0)
    lane = lax.broadcasted_iota(jnp.int32, (8, NB), 1)
    rows = list(rows)
    for p in range(16):
        o = 8 * p
        panel = rows[p]
        cols = [lane_bcast(panel, o + j) for j in range(8)]
        inside = (lane >= o) & (lane < o + 8)
        panel = jnp.where(inside, jnp.where(lane - o == sub, 1.0, 0.0), panel)
        for j in range(8):
            on_pivot = sub == j
            r = 1.0 / sub_bcast(cols[j], j)
            m = cols[j] * r

            def eliminate(v):
                pivot_row = sub_bcast(v, j)
                return jnp.where(on_pivot, pivot_row * r, v - m * pivot_row)

            for q in range(j + 1, 8):
                cols[q] = eliminate(cols[q])
            panel = eliminate(panel)
        rows[p] = panel
        pivots = [sub_bcast(panel, j) for j in range(8)]
        for t in range(15):
            i = (p + 1 + t) % 16
            v = rows[i]
            terms = [lane_bcast(v, o + j) * pivots[j] for j in range(8)]
            while len(terms) > 1:
                terms = [terms[s] + terms[s + 1] for s in range(0, len(terms), 2)]
            rows[i] = jnp.where(inside, 0.0, v) - terms[0]
    return rows


def invert(a_ref):
    nb = K // NB
    blk = lambda k: slice(NB * k, NB * (k + 1))
    for k in range(nb):
        ks = blk(k)
        rows = inverse_128([a_ref[NB * k + 8 * t : NB * k + 8 * t + 8, ks] for t in range(16)])
        diag = jnp.concatenate(rows, axis=0)
        right = {}
        for j in range(nb):
            if j == k:
                right[j] = diag
            else:
                right[j] = jnp.dot(diag, a_ref[ks, blk(j)], precision=HI, preferred_element_type=F32)
        left = {i: a_ref[blk(i), ks] for i in range(nb) if i != k}
        for j in range(nb):
            a_ref[ks, blk(j)] = right[j]
        for s in range(nb - 1):
            i = (k + 1 + s) % nb
            for t in range(nb):
                j = (k + 1 + t) % nb
                u = jnp.dot(left[i], right[j], precision=HI, preferred_element_type=F32)
                if j == k:
                    a_ref[blk(i), ks] = -u
                else:
                    a_ref[blk(i), blk(j)] = a_ref[blk(i), blk(j)] - u


def assemble(where_ref, pieces, out_ref):
    core, y = where_ref[0], where_ref[1]
    for side in range(2):
        half = core if side == 0 else 1 - core
        for d in range(NY):
            part = lax.rem(y + (NY - d), NY)
            row = pl.multiple_of(lax.rem(part, 2) * HALF, HALF)
            col = pl.multiple_of((half * 2 + lax.div(part, 2)) * NB, NB)
            piece = pieces[side * NY + d]
            out_ref[pl.ds(row, HALF), pl.ds(col, NB)] = piece[...].reshape(HALF, NB)


def invert_kernel(where_ref, *refs):
    assemble(where_ref, refs[:8], refs[8])
    invert(refs[8])


def inverse(where, pieces):
    vmem = pl.BlockSpec(memory_space=pltpu.VMEM)
    return pl.pallas_call(
        invert_kernel,
        in_specs=[pl.BlockSpec(memory_space=pltpu.SMEM)] + [vmem] * 8,
        out_specs=vmem,
        out_shape=jax.ShapeDtypeStruct((K, K), F32),
        compiler_params=pltpu.CompilerParams(vmem_limit_bytes=16 << 20),
        cost_estimate=pl.CostEstimate(
            flops=12 * K * K * K, bytes_accessed=8 * K * K * 4, transcendentals=0
        ),
        name="inverse",
    )(where, *pieces)


def finish_kernel(where_ref, inv_ref, *refs):
    pieces = refs[:8]
    x_ref, y_ref, pred_ref, res_hbm = refs[8:12]
    c_ref, res_ref, hi_ref, lo_ref, sem_o = refs[12:]
    assemble(where_ref, pieces, c_ref)
    pred = jnp.dot(inv_ref[...], c_ref[...], precision=HI, preferred_element_type=F32)
    pred_ref[...] = pred
    high = pred.astype(jnp.bfloat16)
    hi_ref[...] = high
    lo_ref[...] = (pred - high.astype(F32)).astype(jnp.bfloat16)
    def store(n):
        rows = pl.ds(pl.multiple_of(n * CHUNK, CHUNK), CHUNK)
        return pltpu.make_async_copy(res_ref.at[rows, :], res_hbm.at[rows, :], sem_o.at[n])

    @pl.loop(0, res_ref.shape[0] // CHUNK)
    def _(n):
        rows = pl.ds(pl.multiple_of(n * CHUNK, CHUNK), CHUNK)
        x = x_ref[rows, :]
        estimate = jnp.dot(x, hi_ref[...], preferred_element_type=F32) + jnp.dot(
            x, lo_ref[...], preferred_element_type=F32
        )
        res_ref[rows, :] = (y_ref[rows, :].astype(F32) - estimate).astype(jnp.bfloat16)
        store(n).start()

    @pl.loop(0, res_ref.shape[0] // CHUNK)
    def _(n):
        store(n).wait()


def finish(where, inv, pieces, x, y):
    rows = x.shape[0]
    vmem = pl.BlockSpec(memory_space=pltpu.VMEM)
    hbm = pl.BlockSpec(memory_space=pl.ANY)
    return pl.pallas_call(
        finish_kernel,
        in_specs=[pl.BlockSpec(memory_space=pltpu.SMEM)] + [vmem] * 11,
        out_specs=(vmem, hbm),
        out_shape=(
            jax.ShapeDtypeStruct((K, K), F32),
            jax.ShapeDtypeStruct((rows, K), jnp.bfloat16),
        ),
        scratch_shapes=[
            pltpu.VMEM((K, K), F32),
            pltpu.VMEM((rows, K), jnp.bfloat16),
            pltpu.VMEM((K, K), jnp.bfloat16),
            pltpu.VMEM((K, K), jnp.bfloat16),
            pltpu.SemaphoreType.DMA((rows // CHUNK,)),
        ],
        compiler_params=pltpu.CompilerParams(vmem_limit_bytes=32 << 20),
        name="finish",
    )(where, inv, *pieces, x, y)


def body(regressors, targets):
    grp = lax.axis_index("grp")
    where = jnp.stack([grp & 1, grp >> 1]).astype(jnp.int32)
    other = [(g, g ^ 1) for g in range(8)]
    along_y = lambda d: [(g, (g + 2 * d) % 8) for g in range(8)]

    send_g, keep_g, after, x = local_sums(where, regressors, regressors, "gram_sums")
    taken_g = lax.ppermute(send_g, "grp", other)
    send_c, keep_c, _, x = local_sums(after, x, targets, "cross_sums")
    taken_c = lax.ppermute(send_c, "grp", other)
    chip = chip_sums(where, keep_g, keep_c, taken_g, taken_c)
    column = chip[0]
    for d in range(1, NY):
        column = column + lax.ppermute(chip[d], "grp", along_y(d))
    by_zx = lax.all_to_all(column, "shard", 0, 0, tiled=True)
    tile = by_zx.sum(axis=0)
    mine = lax.all_to_all(
        jnp.broadcast_to(tile, (NZX, 2, 8, NB)), "shard", 0, 0, tiled=True
    )

    def gather(piece):
        near = [piece] + [lax.ppermute(piece, "grp", along_y(d)) for d in range(1, NY)]
        return near + [lax.ppermute(part, "grp", other) for part in near]

    gram = gather(mine[:, 0])
    cross = gather(mine[:, 1])
    return finish(where, inverse(where, gram), cross, x, targets)


def solution(mesh):
    placed = (P(("grp", "shard"), None), P(("grp", "shard"), None))
    return jax.shard_map(
        body,
        mesh=mesh,
        in_specs=placed,
        out_specs=(P(), P(("grp", "shard"), None)),
        check_vma=False,
    )
```

```python
import functools

import jax
import jax.numpy as jnp
from jax import lax
from jax.experimental import pallas as pl
from jax.experimental.pallas import tpu as pltpu
from jax.sharding import PartitionSpec as P


F32 = jnp.float32
HI = lax.Precision.HIGHEST
K = 512
HALF = 256
NB = 128
CHUNK = 512
NY = 4
NZX = 32
VMEM = pl.BlockSpec(memory_space=pltpu.VMEM)
SMEM = pl.BlockSpec(memory_space=pltpu.SMEM)
INVERSE_COST = pl.CostEstimate(flops=6 * K * K * K, bytes_accessed=4 << 20, transcendentals=0)


def sums_kernel(where_ref, x_ref, *refs):
    send_ref, keep_ref, next_ref, _, acc_ref = refs[-5:]
    z_ref = refs[0] if len(refs) == 6 else x_ref
    next_ref[0] = where_ref[0]
    next_ref[1] = where_ref[1]
    acc_ref[...] = lax.dot_general(
        x_ref[...], z_ref[...], (((0,), (0,)), ((), ())), preferred_element_type=F32
    )
    core = where_ref[0]
    for out_ref, half in ((send_ref, 1 - core), (keep_ref, core)):
        for jj in range(2):
            col = pl.multiple_of(half * HALF + jj * NB, NB)
            for ih in range(2):
                tile = acc_ref[HALF * ih : HALF * (ih + 1), pl.ds(col, NB)]
                out_ref[jj * 2 + ih] = tile.reshape(NZX, 8, NB)


def local_sums(where, name, x, *z):
    out_shape = jax.ShapeDtypeStruct((NY, NZX, 8, NB), F32)
    return pl.pallas_call(
        sums_kernel,
        in_specs=[SMEM] + [VMEM] * (1 + len(z)),
        out_specs=(VMEM, VMEM, SMEM, VMEM),
        out_shape=(
            out_shape,
            out_shape,
            jax.ShapeDtypeStruct((2,), jnp.int32),
            jax.ShapeDtypeStruct(x.shape, x.dtype),
        ),
        input_output_aliases={1: 3},
        scratch_shapes=[pltpu.VMEM((K, K), F32)],
        compiler_params=pltpu.CompilerParams(vmem_limit_bytes=24 << 20),
        cost_estimate=pl.CostEstimate(
            flops=2 * x.shape[0] * K * K, bytes_accessed=8 << 20, transcendentals=0
        ),
        name=name,
    )(where, x, *z)


def chip_kernel(where_ref, keep_g, keep_c, taken_g, taken_c, *out_refs):
    own_ref, half_refs = out_refs[0], out_refs[1:]
    for d in range(NY):
        part = lax.rem(where_ref[1] + d, NY)
        for kind, keep, taken in ((0, keep_g, taken_g), (1, keep_c, taken_c)):
            total = keep[part] + taken[part]
            if d == 0:
                own_ref[:, kind] = total
            else:
                half_refs[2 * d - 2][:, kind] = total[: NZX // 2]
                half_refs[2 * d - 1][:, kind] = total[NZX // 2 :]


def chip_sums(where, *parts):
    half = jax.ShapeDtypeStruct((NZX // 2, 2, 8, NB), F32)
    return pl.pallas_call(
        chip_kernel,
        in_specs=[SMEM] + [VMEM] * 4,
        out_specs=(VMEM,) * 7,
        out_shape=(jax.ShapeDtypeStruct((NZX, 2, 8, NB), F32),) + (half,) * 6,
        compiler_params=pltpu.CompilerParams(vmem_limit_bytes=8 << 20),
        name="chip_sums",
    )(where, *parts)


def column_kernel(own_ref, r1a, r1b, r3a, r3b, out_ref):
    out_ref[: NZX // 2] = own_ref[: NZX // 2] + (r1a[...] + r3a[...])
    out_ref[NZX // 2 :] = own_ref[NZX // 2 :] + (r1b[...] + r3b[...])


def column_sums(*parts):
    return pl.pallas_call(
        column_kernel,
        in_specs=[VMEM] * 5,
        out_specs=VMEM,
        out_shape=jax.ShapeDtypeStruct((NZX, 2, 8, NB), F32),
        compiler_params=pltpu.CompilerParams(vmem_limit_bytes=4 << 20),
        name="column_sums",
    )(*parts)


def half_kernel(where_ref, *refs):
    near, out_ref, next_ref = refs[:NY], refs[NY], refs[NY + 1]
    next_ref[0] = where_ref[0]
    next_ref[1] = where_ref[1]
    for d in range(NY):
        out_ref[lax.rem(where_ref[1] + (NY - d), NY)] = near[d][...]


def join_half(where, near, name):
    return pl.pallas_call(
        half_kernel,
        in_specs=[SMEM] + [VMEM] * NY,
        out_specs=(VMEM, SMEM),
        out_shape=(
            jax.ShapeDtypeStruct((NY, NZX, 8, NB), F32),
            jax.ShapeDtypeStruct((2,), jnp.int32),
        ),
        compiler_params=pltpu.CompilerParams(vmem_limit_bytes=4 << 20),
        name=name,
    )(where, *near)


def lane_bcast(v, c):
    return jnp.broadcast_to(v[:, c : c + 1], (8, NB))


def sub_bcast(v, r):
    return jnp.broadcast_to(v[r : r + 1, :], (8, NB))


def tree_sum(terms):
    while len(terms) > 1:
        terms = [terms[s] + terms[s + 1] for s in range(0, len(terms), 2)]
    return terms[0]


def eliminate_panel(rows, p, mates, zero):
    sub = lax.broadcasted_iota(jnp.int32, (8, NB), 0)
    lane = lax.broadcasted_iota(jnp.int32, (8, NB), 1)
    o = 8 * p
    panel = rows[p]
    cols = [lane_bcast(panel, o + j) + zero for j in range(8)]
    factors = {i: [lane_bcast(rows[i], o + j) for j in range(8)] for i in mates}
    inside = (lane >= o) & (lane < o + 8)
    panel = jnp.where(inside, jnp.where(lane - o == sub, 1.0, 0.0), panel)
    for j in range(0, 8, 2):
        first, second = sub == j, sub == j + 1
        pivots = first | second
        k0, k1 = cols[j], cols[j + 1]
        a, b, c = sub_bcast(k0, j), sub_bcast(k1, j), sub_bcast(k1, j + 1)
        r = 1.0 / (a * c - b * b)
        e0 = jnp.where(first, -c, jnp.where(second, b, k0 * c - k1 * b))
        e1 = jnp.where(first, b, jnp.where(second, -a, k1 * a - k0 * b))

        def eliminate(v):
            v0, v1 = sub_bcast(v, j), sub_bcast(v, j + 1)
            return jnp.where(pivots, 0.0, v) - (e0 * v0 + e1 * v1) * r

        for q in range(j + 2, 8):
            cols[q] = eliminate(cols[q])
        panel = eliminate(panel)
    rows[p] = panel
    by_row = [sub_bcast(panel, j) for j in range(8)]
    for i in mates:
        rows[i] = jnp.where(inside, 0.0, rows[i]) - tree_sum(
            [factors[i][j] * by_row[j] for j in range(8)]
        )


def inverse_128(rows, zero):
    lane = lax.broadcasted_iota(jnp.int32, (8, NB), 1)
    blank = jnp.zeros((8, NB), F32)
    rows = list(rows)
    for p in range(0, 16, 2):
        near = [p + 2, p + 3] if p < 14 else []
        factors = {i: [lane_bcast(rows[i], 8 * p + j) for j in range(16)] for i in near}
        eliminate_panel(rows, p, [p + 1], zero)
        eliminate_panel(rows, p + 1, [p], zero)
        inside = (lane >= 8 * p) & (lane < 8 * p + 16)
        by_row = [sub_bcast(rows[p + j // 8], j % 8) for j in range(16)] if near else []
        for i in near:
            rows[i] = jnp.where(inside, 0.0, rows[i]) - tree_sum(
                [factors[i][j] * by_row[j] for j in range(16)]
            )
        rest = [i % 16 for i in range(p + 2, p + 16) if i % 16 not in near]
        right = jnp.concatenate([rows[i] if i in (p, p + 1) else blank for i in range(16)], axis=0)
        left = jnp.concatenate([jnp.where(inside, rows[i], 0.0) for i in rest], axis=0)
        u = jnp.dot(left, right, precision=HI, preferred_element_type=F32)
        for t, i in enumerate(rest):
            rows[i] = jnp.where(inside, 0.0, rows[i]) - u[8 * t : 8 * t + 8, :]
    return rows


def block(k):
    return slice(NB * k, NB * (k + 1))


def sweep(a_ref, steps, zero):
    nb = K // NB
    for k in steps:
        ks = block(k)
        rows = inverse_128(
            [a_ref[NB * k + 8 * t : NB * k + 8 * t + 8, ks] for t in range(16)], zero
        )
        diag = jnp.concatenate(rows, axis=0)
        right = {}
        for j in range(nb):
            if j == k:
                right[j] = diag
            else:
                right[j] = jnp.dot(
                    diag, a_ref[ks, block(j)], precision=HI, preferred_element_type=F32
                )
        left = {i: a_ref[block(i), ks] for i in range(nb) if i != k}
        for j in range(nb):
            a_ref[ks, block(j)] = right[j]
        for s in range(nb - 1):
            i = (k + 1 + s) % nb
            for t in range(nb):
                j = (k + 1 + t) % nb
                u = jnp.dot(left[i], right[j], precision=HI, preferred_element_type=F32)
                if j == k:
                    a_ref[block(i), ks] = -u
                else:
                    a_ref[block(i), block(j)] = a_ref[block(i), block(j)] - u


def assemble(core, own_ref, other_ref, out_ref):
    for half, ref in ((core, own_ref), (1 - core, other_ref)):
        for part in range(NY):
            rows = slice(HALF * (part % 2), HALF * (part % 2 + 1))
            col = pl.multiple_of((half * 2 + part // 2) * NB, NB)
            out_ref[rows, pl.ds(col, NB)] = ref[part].reshape(HALF, NB)


def zero_of(where_ref):
    return lax.shift_right_logical(where_ref[0], 8).astype(F32)


def scale_by(a_ref, col_scale, row_scale):
    for i in range(K // NB):
        for j in range(K // NB):
            a_ref[block(i), block(j)] = (a_ref[block(i), block(j)] * col_scale(i)) * row_scale(j)


def first_kernel(where_ref, own_ref, other_ref, a_ref, col_ref, row_ref, next_ref):
    next_ref[0] = where_ref[0]
    next_ref[1] = where_ref[1]
    assemble(where_ref[0], own_ref, other_ref, a_ref)
    on_diag = lax.broadcasted_iota(jnp.int32, (NB, NB), 0) == lax.broadcasted_iota(
        jnp.int32, (NB, NB), 1
    )
    for k in range(K // NB):
        diag = jnp.where(on_diag, a_ref[block(k), block(k)], 0.0)
        down = lax.rsqrt(jnp.sum(diag, axis=1, keepdims=True))
        across = lax.rsqrt(jnp.sum(diag, axis=0, keepdims=True))
        col_ref[block(k), :] = jnp.broadcast_to(down, (NB, NB))
        row_ref[:, block(k)] = jnp.broadcast_to(across, (8, NB))
    scale_by(a_ref, lambda i: col_ref[block(i), :], lambda j: row_ref[0:1, block(j)])
    sweep(a_ref, (0, 1), zero_of(where_ref))


def second_kernel(where_ref, a_in, col_ref, row_ref, a_ref):
    a_ref[...] = a_in[...]
    sweep(a_ref, (2, 3), zero_of(where_ref))
    scale_by(a_ref, lambda i: col_ref[block(i), :], lambda j: row_ref[0:1, block(j)])


def inverse_first(where, own, other):
    return pl.pallas_call(
        first_kernel,
        in_specs=[SMEM] + [VMEM] * 2,
        out_specs=(VMEM, VMEM, VMEM, SMEM),
        out_shape=(
            jax.ShapeDtypeStruct((K, K), F32),
            jax.ShapeDtypeStruct((K, NB), F32),
            jax.ShapeDtypeStruct((8, K), F32),
            jax.ShapeDtypeStruct((2,), jnp.int32),
        ),
        compiler_params=pltpu.CompilerParams(vmem_limit_bytes=12 << 20),
        cost_estimate=INVERSE_COST,
        name="inverse_first",
    )(where, own, other)


def inverse_second(where, a, col, row):
    return pl.pallas_call(
        second_kernel,
        in_specs=[SMEM] + [VMEM] * 3,
        out_specs=VMEM,
        out_shape=jax.ShapeDtypeStruct((K, K), F32),
        compiler_params=pltpu.CompilerParams(vmem_limit_bytes=12 << 20),
        cost_estimate=INVERSE_COST,
        name="inverse_second",
    )(where, a, col, row)


def finish_kernel(
    where_ref, inv_ref, own_ref, other_ref, x_ref, y_ref, pred_ref, res_hbm, *scratch
):
    c_ref, res_ref, hi_ref, lo_ref, sem_o = scratch
    assemble(where_ref[0], own_ref, other_ref, c_ref)
    pred = jnp.dot(inv_ref[...], c_ref[...], precision=HI, preferred_element_type=F32)
    pred_ref[...] = pred
    high = pred.astype(jnp.bfloat16)
    hi_ref[...] = high
    lo_ref[...] = (pred - high.astype(F32)).astype(jnp.bfloat16)
    def store(n):
        rows = pl.ds(pl.multiple_of(n * CHUNK, CHUNK), CHUNK)
        return pltpu.make_async_copy(res_ref.at[rows, :], res_hbm.at[rows, :], sem_o.at[n])

    @pl.loop(0, res_ref.shape[0] // CHUNK)
    def _(n):
        rows = pl.ds(pl.multiple_of(n * CHUNK, CHUNK), CHUNK)
        x = x_ref[rows, :]
        estimate = jnp.dot(x, hi_ref[...], preferred_element_type=F32) + jnp.dot(
            x, lo_ref[...], preferred_element_type=F32
        )
        res_ref[rows, :] = (y_ref[rows, :].astype(F32) - estimate).astype(jnp.bfloat16)
        store(n).start()

    @pl.loop(0, res_ref.shape[0] // CHUNK)
    def _(n):
        store(n).wait()


def finish(where, inv, own, other, x, y):
    rows = x.shape[0]
    return pl.pallas_call(
        finish_kernel,
        in_specs=[SMEM] + [VMEM] * 5,
        out_specs=(VMEM, pl.BlockSpec(memory_space=pl.ANY)),
        out_shape=(
            jax.ShapeDtypeStruct((K, K), F32),
            jax.ShapeDtypeStruct((rows, K), jnp.bfloat16),
        ),
        scratch_shapes=[
            pltpu.VMEM((K, K), F32),
            pltpu.VMEM((rows, K), jnp.bfloat16),
            pltpu.VMEM((K, K), jnp.bfloat16),
            pltpu.VMEM((K, K), jnp.bfloat16),
            pltpu.SemaphoreType.DMA((rows // CHUNK,)),
        ],
        compiler_params=pltpu.CompilerParams(vmem_limit_bytes=32 << 20),
        name="finish",
    )(where, inv, own, other, x, y)


def body(regressors, targets):
    grp = lax.axis_index("grp")
    where = jnp.stack([grp & 1, grp >> 1]).astype(jnp.int32)
    other = [(g, g ^ 1) for g in range(8)]
    along_y = lambda d: [(g, (g + 2 * d) % 8) for g in range(8)]

    send_g, keep_g, after, x = local_sums(where, "gram_sums", regressors)
    taken_g = lax.ppermute(send_g, "grp", other)
    send_c, keep_c, _, x = local_sums(after, "cross_sums", x, targets)
    taken_c = lax.ppermute(send_c, "grp", other)
    own, d1a, d1b, d2a, d2b, d3a, d3b = chip_sums(where, keep_g, keep_c, taken_g, taken_c)
    up, down = along_y(1), along_y(3)
    d1a = d1a + lax.ppermute(d2a, "grp", up)
    d3b = d3b + lax.ppermute(d2b, "grp", down)
    column = column_sums(
        own,
        lax.ppermute(d1a, "grp", up),
        lax.ppermute(d1b, "grp", up),
        lax.ppermute(d3a, "grp", down),
        lax.ppermute(d3b, "grp", down),
    )
    by_zx = lax.all_to_all(column, "shard", 0, 0, tiled=True)
    tile = by_zx.sum(axis=0)
    mine = lax.all_to_all(
        jnp.broadcast_to(tile, (NZX, 2, 8, NB)), "shard", 0, 0, tiled=True
    )

    def gather(piece):
        return [piece] + [lax.ppermute(piece, "grp", along_y(d)) for d in range(1, NY)]

    near_g, near_c = gather(mine[:, 0]), gather(mine[:, 1])
    own_g, _ = join_half(where, near_g, "gram_half")
    a, col, row, after = inverse_first(where, own_g, lax.ppermute(own_g, "grp", other))
    own_c, after = join_half(after, near_c, "cross_half")
    other_c = lax.ppermute(own_c, "grp", other)
    inv = inverse_second(after, a, col, row)
    return finish(where, inv, own_c, other_c, x, targets)


def solution(mesh):
    placed = (P(("grp", "shard"), None), P(("grp", "shard"), None))
    return jax.shard_map(
        body,
        mesh=mesh,
        in_specs=placed,
        out_specs=(P(), P(("grp", "shard"), None)),
        check_vma=False,
    )
```

```python
import functools

import jax
import jax.numpy as jnp
from jax import lax
from jax.experimental import pallas as pl
from jax.experimental.pallas import tpu as pltpu
from jax.sharding import PartitionSpec as P


F32 = jnp.float32
HI = lax.Precision.HIGHEST
K = 512
HALF = 256
NB = 128
CHUNK = 512
NY = 4
NZX = 32
VMEM = pl.BlockSpec(memory_space=pltpu.VMEM)
INVERSE_COST = pl.CostEstimate(flops=6 * K * K * K, bytes_accessed=4 << 20, transcendentals=0)


def position():
    grp = lax.axis_index("grp")
    return lax.rem(grp, 2), lax.div(grp, 2)


def sums_kernel(x_ref, *refs):
    send_ref, keep_ref, _, acc_ref = refs[-4:]
    z_ref = refs[0] if len(refs) == 5 else x_ref
    acc_ref[...] = lax.dot_general(
        x_ref[...], z_ref[...], (((0,), (0,)), ((), ())), preferred_element_type=F32
    )
    core, _ = position()
    for out_ref, half in ((send_ref, 1 - core), (keep_ref, core)):
        for jj in range(2):
            col = pl.multiple_of(half * HALF + jj * NB, NB)
            for ih in range(2):
                tile = acc_ref[HALF * ih : HALF * (ih + 1), pl.ds(col, NB)]
                out_ref[jj * 2 + ih] = tile.reshape(NZX, 8, NB)


def local_sums(name, x, *z):
    out_shape = jax.ShapeDtypeStruct((NY, NZX, 8, NB), F32)
    return pl.pallas_call(
        sums_kernel,
        in_specs=[VMEM] * (1 + len(z)),
        out_specs=(VMEM, VMEM, VMEM),
        out_shape=(out_shape, out_shape, jax.ShapeDtypeStruct(x.shape, x.dtype)),
        input_output_aliases={0: 2},
        scratch_shapes=[pltpu.VMEM((K, K), F32)],
        compiler_params=pltpu.CompilerParams(vmem_limit_bytes=24 << 20),
        cost_estimate=pl.CostEstimate(
            flops=2 * x.shape[0] * K * K, bytes_accessed=8 << 20, transcendentals=0
        ),
        name=name,
    )(x, *z)


def chip_kernel(keep_g, keep_c, taken_g, taken_c, *out_refs):
    own_ref, half_refs = out_refs[0], out_refs[1:]
    _, y = position()
    for d in range(NY):
        part = lax.rem(y + d, NY)
        for kind, keep, taken in ((0, keep_g, taken_g), (1, keep_c, taken_c)):
            total = keep[part] + taken[part]
            if d == 0:
                own_ref[:, kind] = total
            else:
                half_refs[2 * d - 2][:, kind] = total[: NZX // 2]
                half_refs[2 * d - 1][:, kind] = total[NZX // 2 :]


def chip_sums(*parts):
    half = jax.ShapeDtypeStruct((NZX // 2, 2, 8, NB), F32)
    return pl.pallas_call(
        chip_kernel,
        in_specs=[VMEM] * 4,
        out_specs=(VMEM,) * 7,
        out_shape=(jax.ShapeDtypeStruct((NZX, 2, 8, NB), F32),) + (half,) * 6,
        compiler_params=pltpu.CompilerParams(vmem_limit_bytes=8 << 20),
        name="chip_sums",
    )(*parts)


def column_kernel(own_ref, r1a, r1b, r3a, r3b, out_ref):
    out_ref[: NZX // 2] = own_ref[: NZX // 2] + (r1a[...] + r3a[...])
    out_ref[NZX // 2 :] = own_ref[NZX // 2 :] + (r1b[...] + r3b[...])


def column_sums(*parts):
    return pl.pallas_call(
        column_kernel,
        in_specs=[VMEM] * 5,
        out_specs=VMEM,
        out_shape=jax.ShapeDtypeStruct((NZX, 2, 8, NB), F32),
        compiler_params=pltpu.CompilerParams(vmem_limit_bytes=4 << 20),
        name="column_sums",
    )(*parts)


def half_kernel(*refs):
    near, out_ref = refs[:NY], refs[-2]
    _, y = position()
    for d in range(NY):
        out_ref[lax.rem(y + (NY - d), NY)] = near[d][...]


def join_half(near, token, name):
    return pl.pallas_call(
        half_kernel,
        in_specs=[VMEM] * (NY + 1),
        out_specs=(VMEM, VMEM),
        out_shape=(
            jax.ShapeDtypeStruct((NY, NZX, 8, NB), F32),
            jax.ShapeDtypeStruct(token.shape, token.dtype),
        ),
        input_output_aliases={NY: 1},
        compiler_params=pltpu.CompilerParams(vmem_limit_bytes=4 << 20),
        name=name,
    )(*near, token)


def lane_bcast(v, c):
    return jnp.broadcast_to(v[:, c : c + 1], (8, NB))


def sub_bcast(v, r):
    return jnp.broadcast_to(v[r : r + 1, :], (8, NB))


def tree_sum(terms):
    while len(terms) > 1:
        terms = [terms[s] + terms[s + 1] for s in range(0, len(terms), 2)]
    return terms[0]


def eliminate_panel(rows, p, mates, zero):
    sub = lax.broadcasted_iota(jnp.int32, (8, NB), 0)
    lane = lax.broadcasted_iota(jnp.int32, (8, NB), 1)
    o = 8 * p
    panel = rows[p]
    cols = [lane_bcast(panel, o + j) + zero for j in range(8)]
    factors = {i: [lane_bcast(rows[i], o + j) for j in range(8)] for i in mates}
    inside = (lane >= o) & (lane < o + 8)
    panel = jnp.where(inside, jnp.where(lane - o == sub, 1.0, 0.0), panel)
    for j in range(0, 8, 2):
        first, second = sub == j, sub == j + 1
        pivots = first | second
        k0, k1 = cols[j], cols[j + 1]
        a, b, c = sub_bcast(k0, j), sub_bcast(k1, j), sub_bcast(k1, j + 1)
        r = 1.0 / (a * c - b * b)
        e0 = jnp.where(first, -c, jnp.where(second, b, k0 * c - k1 * b))
        e1 = jnp.where(first, b, jnp.where(second, -a, k1 * a - k0 * b))

        def eliminate(v):
            v0, v1 = sub_bcast(v, j), sub_bcast(v, j + 1)
            return jnp.where(pivots, 0.0, v) - (e0 * v0 + e1 * v1) * r

        for q in range(j + 2, 8):
            cols[q] = eliminate(cols[q])
        panel = eliminate(panel)
    rows[p] = panel
    by_row = [sub_bcast(panel, j) for j in range(8)]
    for i in mates:
        rows[i] = jnp.where(inside, 0.0, rows[i]) - tree_sum(
            [factors[i][j] * by_row[j] for j in range(8)]
        )


def inverse_128(rows, zero):
    lane = lax.broadcasted_iota(jnp.int32, (8, NB), 1)
    blank = jnp.zeros((8, NB), F32)
    rows = list(rows)
    for p in range(0, 16, 2):
        near = [p + 2, p + 3] if p < 14 else []
        factors = {i: [lane_bcast(rows[i], 8 * p + j) for j in range(16)] for i in near}
        eliminate_panel(rows, p, [p + 1], zero)
        eliminate_panel(rows, p + 1, [p], zero)
        inside = (lane >= 8 * p) & (lane < 8 * p + 16)
        by_row = [sub_bcast(rows[p + j // 8], j % 8) for j in range(16)] if near else []
        for i in near:
            rows[i] = jnp.where(inside, 0.0, rows[i]) - tree_sum(
                [factors[i][j] * by_row[j] for j in range(16)]
            )
        rest = [i % 16 for i in range(p + 2, p + 16) if i % 16 not in near]
        right = jnp.concatenate([rows[i] if i in (p, p + 1) else blank for i in range(16)], axis=0)
        left = jnp.concatenate([jnp.where(inside, rows[i], 0.0) for i in rest], axis=0)
        u = jnp.dot(left, right, precision=HI, preferred_element_type=F32)
        for t, i in enumerate(rest):
            rows[i] = jnp.where(inside, 0.0, rows[i]) - u[8 * t : 8 * t + 8, :]
    return rows


def block(k):
    return slice(NB * k, NB * (k + 1))


def on_diagonal():
    return lax.broadcasted_iota(jnp.int32, (NB, NB), 0) == lax.broadcasted_iota(
        jnp.int32, (NB, NB), 1
    )


def sweep(a_ref, steps):
    nb = K // NB
    zero = lax.shift_right_logical(lax.axis_index("grp"), 8).astype(F32)
    one = on_diagonal().astype(F32)
    for k in steps:
        ks = block(k)
        rows = inverse_128(
            [a_ref[NB * k + 8 * t : NB * k + 8 * t + 8, ks] for t in range(16)], zero
        )
        diag = jnp.concatenate(rows, axis=0)
        a_ref[ks, ks] = one
        right = jnp.dot(diag, a_ref[ks, :], precision=HI, preferred_element_type=F32)
        others = [(k + 1 + t) % nb for t in range(nb - 1)]
        left = jnp.concatenate([a_ref[block(i), ks] for i in others], axis=0)
        a_ref[ks, :] = right
        for i in others:
            a_ref[block(i), ks] = jnp.zeros((NB, NB), F32)
        u = jnp.dot(left, right, precision=HI, preferred_element_type=F32)
        for t, i in enumerate(others):
            a_ref[block(i), :] = a_ref[block(i), :] - u[NB * t : NB * (t + 1), :]


def assemble(core, own_ref, other_ref, out_ref):
    for half, ref in ((core, own_ref), (1 - core, other_ref)):
        for part in range(NY):
            rows = slice(HALF * (part % 2), HALF * (part % 2 + 1))
            col = pl.multiple_of((half * 2 + part // 2) * NB, NB)
            out_ref[rows, pl.ds(col, NB)] = ref[part].reshape(HALF, NB)


def scale_by(a_ref, col_scale, row_scale):
    for i in range(K // NB):
        for j in range(K // NB):
            a_ref[block(i), block(j)] = (a_ref[block(i), block(j)] * col_scale(i)) * row_scale(j)


def first_kernel(own_ref, other_ref, a_ref, col_ref, row_ref):
    core, _ = position()
    assemble(core, own_ref, other_ref, a_ref)
    on_diag = on_diagonal()
    for k in range(K // NB):
        diag = jnp.where(on_diag, a_ref[block(k), block(k)], 0.0)
        down = lax.rsqrt(jnp.sum(diag, axis=1, keepdims=True))
        across = lax.rsqrt(jnp.sum(diag, axis=0, keepdims=True))
        col_ref[block(k), :] = jnp.broadcast_to(down, (NB, NB))
        row_ref[:, block(k)] = jnp.broadcast_to(across, (8, NB))
    scale_by(a_ref, lambda i: col_ref[block(i), :], lambda j: row_ref[0:1, block(j)])
    sweep(a_ref, (0, 1))


def second_kernel(a_in, col_ref, row_ref, a_ref):
    a_ref[...] = a_in[...]
    sweep(a_ref, (2, 3))
    scale_by(a_ref, lambda i: col_ref[block(i), :], lambda j: row_ref[0:1, block(j)])


def inverse_first(own, other):
    return pl.pallas_call(
        first_kernel,
        in_specs=[VMEM] * 2,
        out_specs=(VMEM, VMEM, VMEM),
        out_shape=(
            jax.ShapeDtypeStruct((K, K), F32),
            jax.ShapeDtypeStruct((K, NB), F32),
            jax.ShapeDtypeStruct((8, K), F32),
        ),
        compiler_params=pltpu.CompilerParams(vmem_limit_bytes=12 << 20),
        cost_estimate=INVERSE_COST,
        name="inverse_first",
    )(own, other)


def inverse_second(a, col, row):
    return pl.pallas_call(
        second_kernel,
        in_specs=[VMEM] * 3,
        out_specs=VMEM,
        out_shape=jax.ShapeDtypeStruct((K, K), F32),
        compiler_params=pltpu.CompilerParams(vmem_limit_bytes=12 << 20),
        cost_estimate=INVERSE_COST,
        name="inverse_second",
    )(a, col, row)


def finish_kernel(inv_ref, own_ref, other_ref, x_ref, y_ref, pred_ref, res_hbm, *scratch):
    res_ref, hi_ref, lo_ref, sem_o = scratch
    core, _ = position()
    for half, ref in ((core, own_ref), (1 - core, other_ref)):
        part = [ref[n].reshape(HALF, NB) for n in range(NY)]
        columns = jnp.concatenate(
            [
                jnp.concatenate([part[0], part[2]], axis=1),
                jnp.concatenate([part[1], part[3]], axis=1),
            ],
            axis=0,
        )
        pred_ref[:, pl.ds(pl.multiple_of(half * HALF, HALF), HALF)] = jnp.dot(
            inv_ref[...], columns, precision=HI, preferred_element_type=F32
        )
    pred = pred_ref[...]
    high = pred.astype(jnp.bfloat16)
    hi_ref[...] = high
    lo_ref[...] = (pred - high.astype(F32)).astype(jnp.bfloat16)
    def store(n):
        rows = pl.ds(pl.multiple_of(n * CHUNK, CHUNK), CHUNK)
        return pltpu.make_async_copy(res_ref.at[rows, :], res_hbm.at[rows, :], sem_o.at[n])

    @pl.loop(0, res_ref.shape[0] // CHUNK)
    def _(n):
        rows = pl.ds(pl.multiple_of(n * CHUNK, CHUNK), CHUNK)
        x = x_ref[rows, :]
        estimate = jnp.dot(x, hi_ref[...], preferred_element_type=F32) + jnp.dot(
            x, lo_ref[...], preferred_element_type=F32
        )
        res_ref[rows, :] = (y_ref[rows, :].astype(F32) - estimate).astype(jnp.bfloat16)
        store(n).start()

    @pl.loop(0, res_ref.shape[0] // CHUNK)
    def _(n):
        store(n).wait()


def finish(inv, own, other, x, y):
    rows = x.shape[0]
    return pl.pallas_call(
        finish_kernel,
        in_specs=[VMEM] * 5,
        out_specs=(VMEM, pl.BlockSpec(memory_space=pl.ANY)),
        out_shape=(
            jax.ShapeDtypeStruct((K, K), F32),
            jax.ShapeDtypeStruct((rows, K), jnp.bfloat16),
        ),
        scratch_shapes=[
            pltpu.VMEM((rows, K), jnp.bfloat16),
            pltpu.VMEM((K, K), jnp.bfloat16),
            pltpu.VMEM((K, K), jnp.bfloat16),
            pltpu.SemaphoreType.DMA((rows // CHUNK,)),
        ],
        compiler_params=pltpu.CompilerParams(vmem_limit_bytes=32 << 20),
        name="finish",
    )(inv, own, other, x, y)


def body(regressors, targets):
    other = [(g, g ^ 1) for g in range(8)]
    along_y = lambda d: [(g, (g + 2 * d) % 8) for g in range(8)]

    send_g, keep_g, x = local_sums("gram_sums", regressors)
    taken_g = lax.ppermute(send_g, "grp", other)
    send_c, keep_c, x = local_sums("cross_sums", x, targets)
    taken_c = lax.ppermute(send_c, "grp", other)
    own, d1a, d1b, d2a, d2b, d3a, d3b = chip_sums(keep_g, keep_c, taken_g, taken_c)
    up, down = along_y(1), along_y(3)
    d1a = d1a + lax.ppermute(d2a, "grp", up)
    d3b = d3b + lax.ppermute(d2b, "grp", down)
    column = column_sums(
        own,
        lax.ppermute(d1a, "grp", up),
        lax.ppermute(d1b, "grp", up),
        lax.ppermute(d3a, "grp", down),
        lax.ppermute(d3b, "grp", down),
    )
    by_zx = lax.all_to_all(column, "shard", 0, 0, tiled=True)
    tile = by_zx.sum(axis=0)
    mine = lax.all_to_all(
        jnp.broadcast_to(tile, (NZX, 2, 8, NB)), "shard", 0, 0, tiled=True
    )

    def gather(piece):
        return [piece] + [lax.ppermute(piece, "grp", along_y(d)) for d in range(1, NY)]

    near_g, near_c = gather(mine[:, 0]), gather(mine[:, 1])
    own_g, _ = join_half(near_g, jnp.zeros((8, NB), F32), "gram_half")
    a, col, row = inverse_first(own_g, lax.ppermute(own_g, "grp", other))
    own_c, row = join_half(near_c, row, "cross_half")
    other_c = lax.ppermute(own_c, "grp", other)
    inv = inverse_second(a, col, row)
    return finish(inv, own_c, other_c, x, targets)


def solution(mesh):
    placed = (P(("grp", "shard"), None), P(("grp", "shard"), None))
    return jax.shard_map(
        body,
        mesh=mesh,
        in_specs=placed,
        out_specs=(P(), P(("grp", "shard"), None)),
        check_vma=False,
    )
```

```python
import functools

import jax
import jax.numpy as jnp
from jax import lax
from jax.experimental import pallas as pl
from jax.experimental.pallas import tpu as pltpu
from jax.sharding import PartitionSpec as P


F32 = jnp.float32
HI = lax.Precision.HIGHEST
K = 512
HALF = 256
NB = 128
CHUNK = 768
NY = 4
NZX = 32
VMEM = pl.BlockSpec(memory_space=pltpu.VMEM)
INVERSE_COST = pl.CostEstimate(flops=6 * K * K * K, bytes_accessed=4 << 20, transcendentals=0)


def position():
    grp = lax.axis_index("grp")
    return lax.rem(grp, 2), lax.div(grp, 2)


def sums_kernel(x_ref, *refs):
    send_ref, keep_ref, _, acc_ref = refs[-4:]
    z_ref = refs[0] if len(refs) == 5 else x_ref
    acc_ref[...] = lax.dot_general(
        x_ref[...], z_ref[...], (((0,), (0,)), ((), ())), preferred_element_type=F32
    )
    core, _ = position()
    for out_ref, half in ((send_ref, 1 - core), (keep_ref, core)):
        for jj in range(2):
            col = pl.multiple_of(half * HALF + jj * NB, NB)
            for ih in range(2):
                tile = acc_ref[HALF * ih : HALF * (ih + 1), pl.ds(col, NB)]
                out_ref[jj * 2 + ih] = tile.reshape(NZX, 8, NB)


def local_sums(name, x, *z):
    out_shape = jax.ShapeDtypeStruct((NY, NZX, 8, NB), F32)
    return pl.pallas_call(
        sums_kernel,
        in_specs=[VMEM] * (1 + len(z)),
        out_specs=(VMEM, VMEM, VMEM),
        out_shape=(out_shape, out_shape, jax.ShapeDtypeStruct(x.shape, x.dtype)),
        input_output_aliases={0: 2},
        scratch_shapes=[pltpu.VMEM((K, K), F32)],
        compiler_params=pltpu.CompilerParams(vmem_limit_bytes=24 << 20),
        cost_estimate=pl.CostEstimate(
            flops=2 * x.shape[0] * K * K, bytes_accessed=8 << 20, transcendentals=0
        ),
        name=name,
    )(x, *z)


def chip_kernel(keep_g, keep_c, taken_g, taken_c, *out_refs):
    own_ref, half_refs = out_refs[0], out_refs[1:]
    _, y = position()
    for d in range(NY):
        part = lax.rem(y + d, NY)
        for kind, keep, taken in ((0, keep_g, taken_g), (1, keep_c, taken_c)):
            total = keep[part] + taken[part]
            if d == 0:
                own_ref[:, kind] = total
            else:
                half_refs[2 * d - 2][:, kind] = total[: NZX // 2]
                half_refs[2 * d - 1][:, kind] = total[NZX // 2 :]


def chip_sums(*parts):
    half = jax.ShapeDtypeStruct((NZX // 2, 2, 8, NB), F32)
    return pl.pallas_call(
        chip_kernel,
        in_specs=[VMEM] * 4,
        out_specs=(VMEM,) * 7,
        out_shape=(jax.ShapeDtypeStruct((NZX, 2, 8, NB), F32),) + (half,) * 6,
        compiler_params=pltpu.CompilerParams(vmem_limit_bytes=8 << 20),
        name="chip_sums",
    )(*parts)


def column_kernel(own_ref, r1a, r1b, r3a, r3b, out_ref):
    out_ref[: NZX // 2] = own_ref[: NZX // 2] + (r1a[...] + r3a[...])
    out_ref[NZX // 2 :] = own_ref[NZX // 2 :] + (r1b[...] + r3b[...])


def column_sums(*parts):
    return pl.pallas_call(
        column_kernel,
        in_specs=[VMEM] * 5,
        out_specs=VMEM,
        out_shape=jax.ShapeDtypeStruct((NZX, 2, 8, NB), F32),
        compiler_params=pltpu.CompilerParams(vmem_limit_bytes=4 << 20),
        name="column_sums",
    )(*parts)


def half_kernel(*refs):
    near, out_ref = refs[:NY], refs[-2]
    _, y = position()
    for d in range(NY):
        out_ref[lax.rem(y + (NY - d), NY)] = near[d][...]


def join_half(near, token, name):
    return pl.pallas_call(
        half_kernel,
        in_specs=[VMEM] * (NY + 1),
        out_specs=(VMEM, VMEM),
        out_shape=(
            jax.ShapeDtypeStruct((NY, NZX, 8, NB), F32),
            jax.ShapeDtypeStruct(token.shape, token.dtype),
        ),
        input_output_aliases={NY: 1},
        compiler_params=pltpu.CompilerParams(vmem_limit_bytes=4 << 20),
        name=name,
    )(*near, token)


def lane_bcast(v, c):
    return jnp.broadcast_to(v[:, c : c + 1], (8, NB))


def sub_bcast(v, r):
    return jnp.broadcast_to(v[r : r + 1, :], (8, NB))


def tree_sum(terms):
    while len(terms) > 1:
        terms = [terms[s] + terms[s + 1] for s in range(0, len(terms), 2)]
    return terms[0]


def eliminate_panel(panel, cols, more):
    sub = lax.broadcasted_iota(jnp.int32, (8, NB), 0)
    cols, more = list(cols), list(more)
    for j in range(0, 8, 2):
        first, second = sub == j, sub == j + 1
        pivots = first | second
        k0, k1 = cols[j], cols[j + 1]
        a, b, c = sub_bcast(k0, j), sub_bcast(k1, j), sub_bcast(k1, j + 1)
        r = 1.0 / (a * c - b * b)
        e0 = jnp.where(first, -c, jnp.where(second, b, k0 * c - k1 * b))
        e1 = jnp.where(first, b, jnp.where(second, -a, k1 * a - k0 * b))

        def eliminate(v):
            v0, v1 = sub_bcast(v, j), sub_bcast(v, j + 1)
            return jnp.where(pivots, 0.0, v) - (e0 * v0 + e1 * v1) * r

        for q in range(j + 2, 8):
            cols[q] = eliminate(cols[q])
        more = [eliminate(v) for v in more]
        panel = eliminate(panel)
    return panel, more


def times_rows(factors, by_row):
    return tree_sum([f * r for f, r in zip(factors, by_row)])


def inverse_128(rows, zero):
    sub = lax.broadcasted_iota(jnp.int32, (8, NB), 0)
    lane = lax.broadcasted_iota(jnp.int32, (8, NB), 1)
    blank = jnp.zeros((8, NB), F32)
    rows = list(rows)

    def own_columns(v, o):
        inside = (lane >= o) & (lane < o + 8)
        return jnp.where(inside, jnp.where(lane - o == sub, 1.0, 0.0), v), inside

    def spread(v, o, count):
        return [lane_bcast(v, o + j) for j in range(count)]

    for p in range(0, 16, 2):
        o = 8 * p
        near = [p + 2, p + 3] if p < 14 else []
        one, two = rows[p], rows[p + 1]
        factors = {i: spread(rows[i], o, 16) for i in near}
        one_cols = [v + zero for v in spread(one, o, 16)]
        two_cols = [v + zero for v in spread(two, o, 16)]
        one, in_one = own_columns(one, o)
        one, one_more = eliminate_panel(one, one_cols[:8], one_cols[8:])
        two_own = [
            two_cols[8 + q] - times_rows(two_cols[:8], [sub_bcast(one_more[q], j) for j in range(8)])
            for q in range(8)
        ]
        by_one = [sub_bcast(one, j) for j in range(8)]
        two = jnp.where(in_one, 0.0, two) - times_rows(two_cols[:8], by_one)
        two, in_two = own_columns(two, o + 8)
        two, _ = eliminate_panel(two, two_own, [])
        by_two = [sub_bcast(two, j) for j in range(8)]
        one = jnp.where(in_two, 0.0, one) - times_rows(one_more, by_two)
        rows[p], rows[p + 1] = one, two
        inside = in_one | in_two
        by_row = [sub_bcast(one, j) for j in range(8)] + by_two
        for i in near:
            rows[i] = jnp.where(inside, 0.0, rows[i]) - times_rows(factors[i], by_row)
        rest = [i % 16 for i in range(p + 2, p + 16) if i % 16 not in near]
        right = jnp.concatenate([rows[i] if i in (p, p + 1) else blank for i in range(16)], axis=0)
        left = jnp.concatenate([jnp.where(inside, rows[i], 0.0) for i in rest], axis=0)
        u = jnp.dot(left, right, precision=HI, preferred_element_type=F32)
        for t, i in enumerate(rest):
            rows[i] = jnp.where(inside, 0.0, rows[i]) - u[8 * t : 8 * t + 8, :]
    return rows


def block(k):
    return slice(NB * k, NB * (k + 1))


def on_diagonal():
    return lax.broadcasted_iota(jnp.int32, (NB, NB), 0) == lax.broadcasted_iota(
        jnp.int32, (NB, NB), 1
    )


def sweep(a_ref, steps):
    nb = K // NB
    zero = lax.shift_right_logical(lax.axis_index("grp"), 8).astype(F32)
    one = on_diagonal().astype(F32)
    for k in steps:
        ks = block(k)
        rows = inverse_128(
            [a_ref[NB * k + 8 * t : NB * k + 8 * t + 8, ks] for t in range(16)], zero
        )
        diag = jnp.concatenate(rows, axis=0)
        a_ref[ks, ks] = one
        right = jnp.dot(diag, a_ref[ks, :], precision=HI, preferred_element_type=F32)
        others = [(k + 1 + t) % nb for t in range(nb - 1)]
        left = jnp.concatenate([a_ref[block(i), ks] for i in others], axis=0)
        a_ref[ks, :] = right
        for i in others:
            a_ref[block(i), ks] = jnp.zeros((NB, NB), F32)
        u = jnp.dot(left, right, precision=HI, preferred_element_type=F32)
        for t, i in enumerate(others):
            a_ref[block(i), :] = a_ref[block(i), :] - u[NB * t : NB * (t + 1), :]


def assemble(core, own_ref, other_ref, out_ref):
    for half, ref in ((core, own_ref), (1 - core, other_ref)):
        for part in range(NY):
            rows = slice(HALF * (part % 2), HALF * (part % 2 + 1))
            col = pl.multiple_of((half * 2 + part // 2) * NB, NB)
            out_ref[rows, pl.ds(col, NB)] = ref[part].reshape(HALF, NB)


def scale_by(a_ref, col_scale, row_scale):
    for i in range(K // NB):
        for j in range(K // NB):
            a_ref[block(i), block(j)] = (a_ref[block(i), block(j)] * col_scale(i)) * row_scale(j)


def first_kernel(own_ref, other_ref, a_ref, col_ref, row_ref):
    core, _ = position()
    assemble(core, own_ref, other_ref, a_ref)
    on_diag = on_diagonal()
    for k in range(K // NB):
        diag = jnp.where(on_diag, a_ref[block(k), block(k)], 0.0)
        down = lax.rsqrt(jnp.sum(diag, axis=1, keepdims=True))
        across = lax.rsqrt(jnp.sum(diag, axis=0, keepdims=True))
        col_ref[block(k), :] = jnp.broadcast_to(down, (NB, NB))
        row_ref[:, block(k)] = jnp.broadcast_to(across, (8, NB))
    scale_by(a_ref, lambda i: col_ref[block(i), :], lambda j: row_ref[0:1, block(j)])
    sweep(a_ref, (0, 1))


def second_kernel(_, col_ref, row_ref, a_ref):
    sweep(a_ref, (2, 3))
    scale_by(a_ref, lambda i: col_ref[block(i), :], lambda j: row_ref[0:1, block(j)])


def inverse_first(own, other):
    return pl.pallas_call(
        first_kernel,
        in_specs=[VMEM] * 2,
        out_specs=(VMEM, VMEM, VMEM),
        out_shape=(
            jax.ShapeDtypeStruct((K, K), F32),
            jax.ShapeDtypeStruct((K, NB), F32),
            jax.ShapeDtypeStruct((8, K), F32),
        ),
        compiler_params=pltpu.CompilerParams(vmem_limit_bytes=12 << 20),
        cost_estimate=INVERSE_COST,
        name="inverse_first",
    )(own, other)


def inverse_second(a, col, row):
    return pl.pallas_call(
        second_kernel,
        in_specs=[VMEM] * 3,
        out_specs=VMEM,
        out_shape=jax.ShapeDtypeStruct((K, K), F32),
        input_output_aliases={0: 0},
        compiler_params=pltpu.CompilerParams(vmem_limit_bytes=12 << 20),
        cost_estimate=INVERSE_COST,
        name="inverse_second",
    )(a, col, row)


def finish_kernel(inv_ref, own_ref, other_ref, x_ref, y_ref, pred_hbm, res_hbm, *scratch):
    pred_ref, res_ref, hi_ref, lo_ref, sem_p, sem_o = scratch
    core, _ = position()
    for half, ref in ((core, own_ref), (1 - core, other_ref)):
        part = [ref[n].reshape(HALF, NB) for n in range(NY)]
        columns = jnp.concatenate(
            [
                jnp.concatenate([part[0], part[2]], axis=1),
                jnp.concatenate([part[1], part[3]], axis=1),
            ],
            axis=0,
        )
        pred_ref[:, pl.ds(pl.multiple_of(half * HALF, HALF), HALF)] = jnp.dot(
            inv_ref[...], columns, precision=HI, preferred_element_type=F32
        )
    store_pred = pltpu.make_async_copy(pred_ref, pred_hbm, sem_p)
    store_pred.start()
    pred = pred_ref[...]
    high = pred.astype(jnp.bfloat16)
    hi_ref[...] = high
    lo_ref[...] = (pred - high.astype(F32)).astype(jnp.bfloat16)
    def store(n):
        rows = pl.ds(pl.multiple_of(n * CHUNK, CHUNK), CHUNK)
        return pltpu.make_async_copy(res_ref.at[rows, :], res_hbm.at[rows, :], sem_o.at[n])

    @pl.loop(0, res_ref.shape[0] // CHUNK)
    def _(n):
        rows = pl.ds(pl.multiple_of(n * CHUNK, CHUNK), CHUNK)
        x = x_ref[rows, :]
        estimate = jnp.dot(x, hi_ref[...], preferred_element_type=F32) + jnp.dot(
            x, lo_ref[...], preferred_element_type=F32
        )
        res_ref[rows, :] = (y_ref[rows, :].astype(F32) - estimate).astype(jnp.bfloat16)
        store(n).start()

    @pl.loop(0, res_ref.shape[0] // CHUNK)
    def _(n):
        store(n).wait()

    store_pred.wait()


def finish(inv, own, other, x, y):
    rows = x.shape[0]
    return pl.pallas_call(
        finish_kernel,
        in_specs=[VMEM] * 5,
        out_specs=(pl.BlockSpec(memory_space=pl.ANY),) * 2,
        out_shape=(
            jax.ShapeDtypeStruct((K, K), F32),
            jax.ShapeDtypeStruct((rows, K), jnp.bfloat16),
        ),
        scratch_shapes=[
            pltpu.VMEM((K, K), F32),
            pltpu.VMEM((rows, K), jnp.bfloat16),
            pltpu.VMEM((K, K), jnp.bfloat16),
            pltpu.VMEM((K, K), jnp.bfloat16),
            pltpu.SemaphoreType.DMA,
            pltpu.SemaphoreType.DMA((rows // CHUNK,)),
        ],
        compiler_params=pltpu.CompilerParams(vmem_limit_bytes=32 << 20),
        name="finish",
    )(inv, own, other, x, y)


def body(regressors, targets):
    other = [(g, g ^ 1) for g in range(8)]
    along_y = lambda d: [(g, (g + 2 * d) % 8) for g in range(8)]

    send_g, keep_g, x = local_sums("gram_sums", regressors)
    taken_g = lax.ppermute(send_g, "grp", other)
    send_c, keep_c, x = local_sums("cross_sums", x, targets)
    taken_c = lax.ppermute(send_c, "grp", other)
    own, d1a, d1b, d2a, d2b, d3a, d3b = chip_sums(keep_g, keep_c, taken_g, taken_c)
    up, down = along_y(1), along_y(3)
    d1a = d1a + lax.ppermute(d2a, "grp", up)
    d3b = d3b + lax.ppermute(d2b, "grp", down)
    column = column_sums(
        own,
        lax.ppermute(d1a, "grp", up),
        lax.ppermute(d1b, "grp", up),
        lax.ppermute(d3a, "grp", down),
        lax.ppermute(d3b, "grp", down),
    )
    by_zx = lax.all_to_all(column, "shard", 0, 0, tiled=True)
    tile = by_zx.sum(axis=0)
    mine = lax.all_to_all(
        jnp.broadcast_to(tile, (NZX, 2, 8, NB)), "shard", 0, 0, tiled=True
    )

    def gather(piece):
        return [piece] + [lax.ppermute(piece, "grp", along_y(d)) for d in range(1, NY)]

    near_g, near_c = gather(mine[:, 0]), gather(mine[:, 1])
    own_g, _ = join_half(near_g, jnp.zeros((8, NB), F32), "gram_half")
    a, col, row = inverse_first(own_g, lax.ppermute(own_g, "grp", other))
    own_c, row = join_half(near_c, row, "cross_half")
    other_c = lax.ppermute(own_c, "grp", other)
    inv = inverse_second(a, col, row)
    return finish(inv, own_c, other_c, x, targets)


def solution(mesh):
    placed = (P(("grp", "shard"), None), P(("grp", "shard"), None))
    return jax.shard_map(
        body,
        mesh=mesh,
        in_specs=placed,
        out_specs=(P(), P(("grp", "shard"), None)),
        check_vma=False,
    )
```

```python
import functools

import jax
import jax.numpy as jnp
from jax import lax
from jax.experimental import pallas as pl
from jax.experimental.pallas import tpu as pltpu
from jax.sharding import PartitionSpec as P


F32 = jnp.float32
HI = lax.Precision.HIGHEST
K = 512
HALF = 256
NB = 128
CHUNK = 768
NY = 4
NZX = 32
VMEM = pl.BlockSpec(memory_space=pltpu.VMEM)
INVERSE_COST = pl.CostEstimate(flops=6 * K * K * K, bytes_accessed=4 << 20, transcendentals=0)


def position():
    grp = lax.axis_index("grp")
    return lax.rem(grp, 2), lax.div(grp, 2)


def sums_kernel(x_ref, *refs):
    send_ref, keep_ref, _, acc_ref = refs[-4:]
    z_ref = refs[0] if len(refs) == 5 else x_ref
    acc_ref[...] = lax.dot_general(
        x_ref[...], z_ref[...], (((0,), (0,)), ((), ())), preferred_element_type=F32
    )
    core, _ = position()
    for out_ref, half in ((send_ref, 1 - core), (keep_ref, core)):
        for jj in range(2):
            col = pl.multiple_of(half * HALF + jj * NB, NB)
            for ih in range(2):
                tile = acc_ref[HALF * ih : HALF * (ih + 1), pl.ds(col, NB)]
                out_ref[jj * 2 + ih] = tile.reshape(NZX, 8, NB)


def local_sums(name, x, *z):
    out_shape = jax.ShapeDtypeStruct((NY, NZX, 8, NB), F32)
    return pl.pallas_call(
        sums_kernel,
        in_specs=[VMEM] * (1 + len(z)),
        out_specs=(VMEM, VMEM, VMEM),
        out_shape=(out_shape, out_shape, jax.ShapeDtypeStruct(x.shape, x.dtype)),
        input_output_aliases={0: 2},
        scratch_shapes=[pltpu.VMEM((K, K), F32)],
        compiler_params=pltpu.CompilerParams(vmem_limit_bytes=24 << 20),
        cost_estimate=pl.CostEstimate(
            flops=2 * x.shape[0] * K * K, bytes_accessed=8 << 20, transcendentals=0
        ),
        name=name,
    )(x, *z)


def chip_kernel(keep_g, keep_c, taken_g, taken_c, *out_refs):
    own_ref, half_refs = out_refs[0], out_refs[1:]
    _, y = position()
    for d in range(NY):
        part = lax.rem(y + d, NY)
        for kind, keep, taken in ((0, keep_g, taken_g), (1, keep_c, taken_c)):
            total = keep[part] + taken[part]
            if d == 0:
                own_ref[:, kind] = total
            else:
                half_refs[2 * d - 2][:, kind] = total[: NZX // 2]
                half_refs[2 * d - 1][:, kind] = total[NZX // 2 :]


def chip_sums(*parts):
    half = jax.ShapeDtypeStruct((NZX // 2, 2, 8, NB), F32)
    return pl.pallas_call(
        chip_kernel,
        in_specs=[VMEM] * 4,
        out_specs=(VMEM,) * 7,
        out_shape=(jax.ShapeDtypeStruct((NZX, 2, 8, NB), F32),) + (half,) * 6,
        compiler_params=pltpu.CompilerParams(vmem_limit_bytes=8 << 20),
        name="chip_sums",
    )(*parts)


def column_kernel(own_ref, r1a, r1b, r3a, r3b, out_ref):
    out_ref[: NZX // 2] = own_ref[: NZX // 2] + (r1a[...] + r3a[...])
    out_ref[NZX // 2 :] = own_ref[NZX // 2 :] + (r1b[...] + r3b[...])


def column_sums(*parts):
    return pl.pallas_call(
        column_kernel,
        in_specs=[VMEM] * 5,
        out_specs=VMEM,
        out_shape=jax.ShapeDtypeStruct((NZX, 2, 8, NB), F32),
        compiler_params=pltpu.CompilerParams(vmem_limit_bytes=4 << 20),
        name="column_sums",
    )(*parts)


def half_kernel(*refs):
    near, out_ref = refs[:NY], refs[-2]
    _, y = position()
    for d in range(NY):
        out_ref[lax.rem(y + (NY - d), NY)] = near[d][...]


def join_half(near, token, name):
    return pl.pallas_call(
        half_kernel,
        in_specs=[VMEM] * (NY + 1),
        out_specs=(VMEM, VMEM),
        out_shape=(
            jax.ShapeDtypeStruct((NY, NZX, 8, NB), F32),
            jax.ShapeDtypeStruct(token.shape, token.dtype),
        ),
        input_output_aliases={NY: 1},
        compiler_params=pltpu.CompilerParams(vmem_limit_bytes=4 << 20),
        name=name,
    )(*near, token)


def lane_bcast(v, c):
    return jnp.broadcast_to(v[:, c : c + 1], (8, NB))


def sub_bcast(v, r):
    return jnp.broadcast_to(v[r : r + 1, :], (8, NB))


def tree_sum(terms):
    while len(terms) > 1:
        terms = [terms[s] + terms[s + 1] for s in range(0, len(terms), 2)]
    return terms[0]


def eliminate_panel(panel, cols, more):
    sub = lax.broadcasted_iota(jnp.int32, (8, NB), 0)
    cols, more = list(cols), list(more)
    for j in range(0, 8, 2):
        first, second = sub == j, sub == j + 1
        pivots = first | second
        k0, k1 = cols[j], cols[j + 1]
        a, b, c = sub_bcast(k0, j), sub_bcast(k1, j), sub_bcast(k1, j + 1)
        r = 1.0 / (a * c - b * b)
        e0 = jnp.where(first, -c, jnp.where(second, b, k0 * c - k1 * b))
        e1 = jnp.where(first, b, jnp.where(second, -a, k1 * a - k0 * b))

        def eliminate(v):
            v0, v1 = sub_bcast(v, j), sub_bcast(v, j + 1)
            return jnp.where(pivots, 0.0, v) - (e0 * v0 + e1 * v1) * r

        for q in range(j + 2, 8):
            cols[q] = eliminate(cols[q])
        more = [eliminate(v) for v in more]
        panel = eliminate(panel)
    return panel, more


def times_rows(factors, by_row):
    return tree_sum([f * r for f, r in zip(factors, by_row)])


def inverse_128(rows, zero):
    sub = lax.broadcasted_iota(jnp.int32, (8, NB), 0)
    lane = lax.broadcasted_iota(jnp.int32, (8, NB), 1)
    blank = jnp.zeros((8, NB), F32)
    rows = list(rows)

    def own_columns(v, o):
        inside = (lane >= o) & (lane < o + 8)
        return jnp.where(inside, jnp.where(lane - o == sub, 1.0, 0.0), v), inside

    def spread(v, o, count):
        return [lane_bcast(v, o + j) for j in range(count)]

    for p in range(0, 16, 2):
        o = 8 * p
        near = [p + 2, p + 3] if p < 14 else []
        one, two = rows[p], rows[p + 1]
        factors = {i: spread(rows[i], o, 16) for i in near}
        one_cols = [v + zero for v in spread(one, o, 16)]
        two_cols = [v + zero for v in spread(two, o, 16)]
        one, in_one = own_columns(one, o)
        one, one_more = eliminate_panel(one, one_cols[:8], one_cols[8:])
        two_own = [
            two_cols[8 + q] - times_rows(two_cols[:8], [sub_bcast(one_more[q], j) for j in range(8)])
            for q in range(8)
        ]
        by_one = [sub_bcast(one, j) for j in range(8)]
        two = jnp.where(in_one, 0.0, two) - times_rows(two_cols[:8], by_one)
        two, in_two = own_columns(two, o + 8)
        two, _ = eliminate_panel(two, two_own, [])
        by_two = [sub_bcast(two, j) for j in range(8)]
        one = jnp.where(in_two, 0.0, one) - times_rows(one_more, by_two)
        rows[p], rows[p + 1] = one, two
        inside = in_one | in_two
        by_row = [sub_bcast(one, j) for j in range(8)] + by_two
        for i in near:
            rows[i] = jnp.where(inside, 0.0, rows[i]) - times_rows(factors[i], by_row)
        rest = [i % 16 for i in range(p + 2, p + 16) if i % 16 not in near]
        right = jnp.concatenate([rows[i] if i in (p, p + 1) else blank for i in range(16)], axis=0)
        left = jnp.concatenate([jnp.where(inside, rows[i], 0.0) for i in rest], axis=0)
        u = jnp.dot(left, right, precision=HI, preferred_element_type=F32)
        for t, i in enumerate(rest):
            rows[i] = jnp.where(inside, 0.0, rows[i]) - u[8 * t : 8 * t + 8, :]
    return rows


def block(k):
    return slice(NB * k, NB * (k + 1))


def on_diagonal():
    return lax.broadcasted_iota(jnp.int32, (NB, NB), 0) == lax.broadcasted_iota(
        jnp.int32, (NB, NB), 1
    )


def sweep(a_ref, steps):
    nb = K // NB
    zero = lax.shift_right_logical(lax.axis_index("grp"), 8).astype(F32)
    one = on_diagonal().astype(F32)
    for k in steps:
        ks = block(k)
        rows = inverse_128(
            [a_ref[NB * k + 8 * t : NB * k + 8 * t + 8, ks] for t in range(16)], zero
        )
        diag = jnp.concatenate(rows, axis=0)
        a_ref[ks, ks] = one
        right = jnp.dot(diag, a_ref[ks, :], precision=HI, preferred_element_type=F32)
        others = [(k + 1 + t) % nb for t in range(nb - 1)]
        left = jnp.concatenate([a_ref[block(i), ks] for i in others], axis=0)
        a_ref[ks, :] = right
        for i in others:
            a_ref[block(i), ks] = jnp.zeros((NB, NB), F32)
        u = jnp.dot(left, right, precision=HI, preferred_element_type=F32)
        for t, i in enumerate(others):
            a_ref[block(i), :] = a_ref[block(i), :] - u[NB * t : NB * (t + 1), :]


def assemble(core, own_ref, other_ref, out_ref):
    for half, ref in ((core, own_ref), (1 - core, other_ref)):
        for part in range(NY):
            rows = slice(HALF * (part % 2), HALF * (part % 2 + 1))
            col = pl.multiple_of((half * 2 + part // 2) * NB, NB)
            out_ref[rows, pl.ds(col, NB)] = ref[part].reshape(HALF, NB)


def scale_by(a_ref, col_scale, row_scale):
    for i in range(K // NB):
        for j in range(K // NB):
            a_ref[block(i), block(j)] = (a_ref[block(i), block(j)] * col_scale(i)) * row_scale(j)


def first_kernel(own_ref, other_ref, a_ref, col_ref, row_ref):
    core, _ = position()
    assemble(core, own_ref, other_ref, a_ref)
    on_diag = on_diagonal()
    for k in range(K // NB):
        diag = jnp.where(on_diag, a_ref[block(k), block(k)], 0.0)
        down = lax.rsqrt(jnp.sum(diag, axis=1, keepdims=True))
        across = lax.rsqrt(jnp.sum(diag, axis=0, keepdims=True))
        col_ref[block(k), :] = jnp.broadcast_to(down, (NB, NB))
        row_ref[:, block(k)] = jnp.broadcast_to(across, (8, NB))
    scale_by(a_ref, lambda i: col_ref[block(i), :], lambda j: row_ref[0:1, block(j)])
    sweep(a_ref, (0, 1, 2))


def second_kernel(_, col_ref, row_ref, a_ref):
    sweep(a_ref, (3,))
    scale_by(a_ref, lambda i: col_ref[block(i), :], lambda j: row_ref[0:1, block(j)])


def inverse_first(own, other):
    return pl.pallas_call(
        first_kernel,
        in_specs=[VMEM] * 2,
        out_specs=(VMEM, VMEM, VMEM),
        out_shape=(
            jax.ShapeDtypeStruct((K, K), F32),
            jax.ShapeDtypeStruct((K, NB), F32),
            jax.ShapeDtypeStruct((8, K), F32),
        ),
        compiler_params=pltpu.CompilerParams(vmem_limit_bytes=12 << 20),
        cost_estimate=INVERSE_COST,
        name="inverse_first",
    )(own, other)


def inverse_second(a, col, row):
    return pl.pallas_call(
        second_kernel,
        in_specs=[VMEM] * 3,
        out_specs=VMEM,
        out_shape=jax.ShapeDtypeStruct((K, K), F32),
        input_output_aliases={0: 0},
        compiler_params=pltpu.CompilerParams(vmem_limit_bytes=12 << 20),
        cost_estimate=INVERSE_COST,
        name="inverse_second",
    )(a, col, row)


def finish_kernel(inv_ref, own_ref, other_ref, x_ref, y_ref, pred_hbm, res_hbm, *scratch):
    pred_ref, res_ref, hi_ref, lo_ref, sem_p, sem_o = scratch
    core, _ = position()
    for half, ref in ((core, own_ref), (1 - core, other_ref)):
        part = [ref[n].reshape(HALF, NB) for n in range(NY)]
        columns = jnp.concatenate(
            [
                jnp.concatenate([part[0], part[2]], axis=1),
                jnp.concatenate([part[1], part[3]], axis=1),
            ],
            axis=0,
        )
        pred_ref[:, pl.ds(pl.multiple_of(half * HALF, HALF), HALF)] = jnp.dot(
            inv_ref[...], columns, precision=HI, preferred_element_type=F32
        )
    store_pred = pltpu.make_async_copy(pred_ref, pred_hbm, sem_p)
    store_pred.start()
    pred = pred_ref[...]
    high = pred.astype(jnp.bfloat16)
    hi_ref[...] = high
    lo_ref[...] = (pred - high.astype(F32)).astype(jnp.bfloat16)
    def store(n):
        rows = pl.ds(pl.multiple_of(n * CHUNK, CHUNK), CHUNK)
        return pltpu.make_async_copy(res_ref.at[rows, :], res_hbm.at[rows, :], sem_o.at[n])

    @pl.loop(0, res_ref.shape[0] // CHUNK)
    def _(n):
        rows = pl.ds(pl.multiple_of(n * CHUNK, CHUNK), CHUNK)
        x = x_ref[rows, :]
        estimate = jnp.dot(x, hi_ref[...], preferred_element_type=F32) + jnp.dot(
            x, lo_ref[...], preferred_element_type=F32
        )
        res_ref[rows, :] = (y_ref[rows, :].astype(F32) - estimate).astype(jnp.bfloat16)
        store(n).start()

    @pl.loop(0, res_ref.shape[0] // CHUNK)
    def _(n):
        store(n).wait()

    store_pred.wait()


def finish(inv, own, other, x, y):
    rows = x.shape[0]
    return pl.pallas_call(
        finish_kernel,
        in_specs=[VMEM] * 5,
        out_specs=(pl.BlockSpec(memory_space=pl.ANY),) * 2,
        out_shape=(
            jax.ShapeDtypeStruct((K, K), F32),
            jax.ShapeDtypeStruct((rows, K), jnp.bfloat16),
        ),
        scratch_shapes=[
            pltpu.VMEM((K, K), F32),
            pltpu.VMEM((rows, K), jnp.bfloat16),
            pltpu.VMEM((K, K), jnp.bfloat16),
            pltpu.VMEM((K, K), jnp.bfloat16),
            pltpu.SemaphoreType.DMA,
            pltpu.SemaphoreType.DMA((rows // CHUNK,)),
        ],
        compiler_params=pltpu.CompilerParams(vmem_limit_bytes=32 << 20),
        name="finish",
    )(inv, own, other, x, y)


def body(regressors, targets):
    other = [(g, g ^ 1) for g in range(8)]
    along_y = lambda d: [(g, (g + 2 * d) % 8) for g in range(8)]

    send_g, keep_g, x = local_sums("gram_sums", regressors)
    taken_g = lax.ppermute(send_g, "grp", other)
    send_c, keep_c, x = local_sums("cross_sums", x, targets)
    taken_c = lax.ppermute(send_c, "grp", other)
    own, d1a, d1b, d2a, d2b, d3a, d3b = chip_sums(keep_g, keep_c, taken_g, taken_c)
    up, down = along_y(1), along_y(3)
    d1a = d1a + lax.ppermute(d2a, "grp", up)
    d3b = d3b + lax.ppermute(d2b, "grp", down)
    column = column_sums(
        own,
        lax.ppermute(d1a, "grp", up),
        lax.ppermute(d1b, "grp", up),
        lax.ppermute(d3a, "grp", down),
        lax.ppermute(d3b, "grp", down),
    )
    by_zx = lax.all_to_all(column, "shard", 0, 0, tiled=True)
    tile = by_zx.sum(axis=0)
    mine = lax.all_to_all(
        jnp.broadcast_to(tile, (NZX, 2, 8, NB)), "shard", 0, 0, tiled=True
    )

    def gather(piece):
        return [piece] + [lax.ppermute(piece, "grp", along_y(d)) for d in range(1, NY)]

    near_g, near_c = gather(mine[:, 0]), gather(mine[:, 1])
    own_g, _ = join_half(near_g, jnp.zeros((8, NB), F32), "gram_half")
    a, col, row = inverse_first(own_g, lax.ppermute(own_g, "grp", other))
    own_c, row = join_half(near_c, row, "cross_half")
    other_c = lax.ppermute(own_c, "grp", other)
    inv = inverse_second(a, col, row)
    return finish(inv, own_c, other_c, x, targets)


def solution(mesh):
    placed = (P(("grp", "shard"), None), P(("grp", "shard"), None))
    return jax.shard_map(
        body,
        mesh=mesh,
        in_specs=placed,
        out_specs=(P(), P(("grp", "shard"), None)),
        check_vma=False,
    )
```
